256 devices in a mesh: dp: 8 (over z), vocab: 32 (over y, x, core).
Axes of the slice: x: 4, y: 4, z: 8, core: 2. Of those that a mesh axis runs over, the one named last changes fastest.
Arguments:
- hidden: bfloat16 [5120, 4096], P(('dp', 'vocab')), may hold values from -192 to 192, as said below
- out_weight: bfloat16 [4096, 81920], P('dp', 'vocab'), may hold values from -0.09375 to 0.09375
- labels: int32 [5120], P('dp'), may hold values from 0 to 81919
- text_mask: int32 [5120], P('dp'), may hold values from 0 to 1, as said below
Outputs:
- token_loss: float32 [5120], P('dp')
- mean_loss: float32 [], replicated
The draws below stay inside these ranges and needn't reach their ends.
Inputs may be any that keep to these rules, and one draw needn't show every extreme that they name: The hidden states are of moderate size in most rows, possibly larger in a few. `text_mask`: vision and text tokens come in runs of 16 aligned tokens.
All inputs are finite; a program needn't handle non-finite values.
Results may differ from the reference program's by a relative error of at most 0.0003.
Values may be sent and summed in bfloat16 or wider, within the bound.
A program may use at most 128 MiB of HBM per device.

```python
import jax
import jax.numpy as jnp
from jax import lax

D = 4096
TOK_GROUP = 640
VOCAB = 81920
TOKENS = 5120
N_DP = 8


def draw_hidden(key, part):
    values = 3.0 * jax.random.truncated_normal(key, -4.0, 4.0, (TOKENS, D), jnp.float32)
    return values.astype(jnp.bfloat16)


def draw_text_mask(key, part):
    blocks = TOKENS // 16
    group_index = jnp.arange(blocks) * 16 // (TOKENS // N_DP)
    thresh = 25 + 50 * group_index // max(N_DP - 1, 1)
    rolled = jax.random.randint(key, (blocks,), 0, 100)
    is_text = (rolled < thresh).astype(jnp.int32)
    return jnp.repeat(is_text, 16)


def plant(result, rng, least, high):
    place = [jax.random.randint(jax.random.fold_in(rng, axis), (), 0, length) for axis, length in enumerate(result.shape)]
    widest = result.shape.index(max(result.shape))
    next_to = place[:widest] + [(place[widest] + 1) % result.shape[widest]] + place[widest + 1:]
    return result.at[tuple(place)].set(least).at[tuple(next_to)].set(high)


def steps_of(key, dims, split, least, top_value):
    def one(dim, parts):
        heights = jax.random.uniform(jax.random.fold_in(jax.random.fold_in(key, 6), dim), (parts,), jnp.float32, least / len(split), top_value / len(split))
        return jnp.repeat(jnp.exp(heights), dims[dim] // parts).reshape((-1,) + (1,) * (len(dims) - dim - 1))

    factor_of = one(*split[0])
    for cut in split[1:]:
        factor_of = factor_of * one(*cut)
    return factor_of


def centred(stream_key, dims, width, most, pieces=(), kind=jnp.bfloat16):
    drawn = width * jax.random.normal(stream_key, dims, jnp.float32)
    if pieces:
        drawn = drawn * steps_of(stream_key, dims, pieces, -0.22, 0.18)
    return jnp.clip(drawn, -most, most).astype(kind)


def setup_inputs(seed: int = 0) -> dict:
    key_of = jax.random.split(jax.random.key(seed), 5)
    hidden = draw_hidden(jax.random.fold_in(key_of[4], 71), 0)
    out_weight = centred(key_of[1], (D, VOCAB), D ** -0.5, 0.09375, ((0, 8), (1, 32)))
    labels = plant(jax.random.randint(key_of[2], (TOKENS,), 0, VOCAB), jax.random.fold_in(key_of[2], 1), 0, VOCAB - 1).astype(jnp.int32)
    text_mask = draw_text_mask(jax.random.fold_in(key_of[4], 71), 0)
    return {"hidden": hidden, "out_weight": out_weight, "labels": labels, "text_mask": text_mask}


def reference(hidden, out_weight, labels, text_mask):
    columns = jnp.arange(VOCAB, dtype=jnp.int32)

    def per_group(operand):
        states, targets = operand
        logits = jnp.dot(states, out_weight, preferred_element_type=jnp.float32)
        row_top = jnp.max(logits, axis=1)
        exp_total = jnp.sum(jnp.exp(logits - row_top[:, None]), axis=1)
        log_total = row_top + jnp.log(exp_total)
        picked = jnp.sum(jnp.where(columns[None, :] == targets[:, None], logits, jnp.float32(0.0)), axis=1)
        return log_total - picked

    losses = lax.map(per_group, (hidden.reshape(-1, TOK_GROUP, D), labels.reshape(-1, TOK_GROUP))).reshape(-1)
    weights_text = text_mask.astype(jnp.float32)
    token_loss = weights_text * losses
    tally = jnp.sum(weights_text)
    mean_loss = jnp.sum(token_loss) / jnp.maximum(tally, jnp.float32(1.0))
    return token_loss, mean_loss
```

```python
import jax
import jax.numpy as jnp
from jax import lax
from jax.experimental import pallas as pl
from jax.experimental.pallas import tpu as pltpu
from jax.sharding import PartitionSpec as P

NZ, NY, NX, NC = 8, 4, 4, 2
ROWS = 20
D = 4096
KROWS = D // NZ
BLOCK = 640
CH = 128
NQ = BLOCK // CH
GROUP = 8 * ROWS
TOK = NZ * GROUP
SLOTS = 64
LEAST = float(jnp.finfo(jnp.float32).min)
MT = 320


def main_kernel(
    h_ref, w_ref, lab_ref, out_ref,
    raw, act, wbuf, labs, labcol, stage, m_ref, s_ref, p_ref,
    hrecv, hsend, wrecv, wsend, lrecv, lsend, local_sem,
):
    z = lax.axis_index("dp")
    v = lax.axis_index("vocab")
    c = v % 2
    x = (v // 2) % 4
    y = v // 8
    yb = y % 2
    xp, xm = (x + 1) % 4, (x + 3) % 4
    zp, zm = (z + 1) % 8, (z + 7) % 8
    ypair = y + 1 - 2 * yb
    ystar = (y + 2 * yb + 3) % 4

    def dev(zz, yy, xx, cc):
        return {"dp": zz, "vocab": (yy * 4 + xx) * 2 + cc}

    bar = pltpu.get_barrier_semaphore()

    def greet(d):
        pl.semaphore_signal(bar, inc=1, device_id=d, device_id_type=pl.DeviceIdType.MESH)

    @pl.loop(1, 8)
    def _(k):
        greet(dev((z + k) % 8, y, x, c))

    @pl.loop(0, 8)
    def _(k):
        greet(dev((z + k) % 8, y, x, 1 - c))

    greet(dev(z, y, xp, c))
    greet(dev(z, y, xm, c))
    greet(dev(z, ypair, x, c))
    greet(dev(z, ystar, x, c))
    pl.semaphore_wait(bar, 19)

    def slot_of(zs, xs, b):
        return (zs * 4 + xs) * 2 + b

    def h_copy(slot, d):
        return pltpu.make_async_remote_copy(
            src_ref=raw.at[slot], dst_ref=raw.at[slot], send_sem=hsend, recv_sem=hrecv.at[slot],
            device_id=d, device_id_type=pl.DeviceIdType.MESH)

    def h_wait(slot):
        pltpu.make_async_copy(raw.at[slot], raw.at[slot], hrecv.at[slot]).wait()

    to_zp, to_zm = dev(zp, y, x, c), dev(zm, y, x, c)
    to_xp, to_xm = dev(z, y, xp, c), dev(z, y, xm, c)
    to_yp, to_ys = dev(z, ypair, x, c), dev(z, ystar, x, c)
    to_core = dev(z, y, x, 1 - c)

    def z_of(d):
        k = (d + 1) // 2
        return (z + jnp.where(d % 2 == 1, 8 - k, k)) % 8

    def w_at(q, zs, side):
        return wbuf.at[q, pl.ds(pl.multiple_of(zs * KROWS, KROWS), KROWS), pl.ds(side * CH, CH)]

    def w_wait(q, zs, side):
        pltpu.make_async_copy(w_at(q, zs, side), w_at(q, zs, side), wrecv.at[q, zs, side]).wait()

    def w_send(q, zs, side, to_side, d):
        pltpu.make_async_remote_copy(
            src_ref=w_at(q, zs, side), dst_ref=w_at(q, zs, to_side), send_sem=wsend,
            recv_sem=wrecv.at[q, zs, to_side], device_id=d, device_id_type=pl.DeviceIdType.MESH).start()

    tcore = z % 2
    selfish = jnp.logical_and(z // 4 == c, tcore == c)

    def w_first(q):
        @pl.loop(0, 4)
        def _(j):
            p = 4 * c + j
            src = w_ref.at[:, pl.ds(pl.multiple_of(j * BLOCK + q * CH, CH), CH)]
            mine = jnp.logical_and(p == z, tcore == c)

            @pl.when(mine)
            def _():
                pltpu.make_async_copy(src, w_at(q, z, 0), wrecv.at[q, z, 0]).start()

            @pl.when(jnp.logical_not(mine))
            def _():
                pltpu.make_async_remote_copy(
                    src_ref=src, dst_ref=w_at(q, z, 0), send_sem=wsend, recv_sem=wrecv.at[q, z, 0],
                    device_id=dev(p, y, x, tcore), device_id_type=pl.DeviceIdType.MESH).start()

    own_slot = slot_of(z, x, yb)
    own = pltpu.make_async_copy(h_ref, raw.at[own_slot], local_sem)
    own.start()

    own.wait()

    same = (c + z) % 2

    def w_z(n):
        a, b = ((0, 1), (2, 7), (6, 3), (4, 5))[n]
        return (z + jnp.where(same == 0, a, b)) % 8

    def step_a(d):
        zs = z_of(d)
        slot = slot_of(zs, x, yb)

        @pl.when(d > 0)
        def _():
            h_wait(slot)

        even = zs % 2 == 0
        odd_d = d % 2 == 1
        up = (d == 0) | (odd_d & (d <= 3)) | ((d == 5) & even)
        down = (d == 0) | (jnp.logical_not(odd_d) & (d <= 4)) | ((d == 6) & jnp.logical_not(even))

        @pl.when(up)
        def _():
            h_copy(slot, to_zp).start()

        @pl.when(down)
        def _():
            h_copy(slot, to_zm).start()

        h_copy(slot, to_xp).start()
        h_copy(slot, to_xm).start()
        h_copy(slot, to_yp).start()

    def step_b(d):
        zs = z_of(d)
        even = zs % 2 == 0
        s1, s2, s3 = slot_of(zs, xm, yb), slot_of(zs, xp, yb), slot_of(zs, x, 1 - yb)
        h_wait(s1)

        @pl.when(even)
        def _():
            h_copy(s1, to_xp).start()

        @pl.when(c == 0)
        def _():
            h_copy(s1, to_yp).start()

        h_wait(s2)

        @pl.when(jnp.logical_not(even))
        def _():
            h_copy(s2, to_xm).start()

        @pl.when(c == 0)
        def _():
            h_copy(s2, to_yp).start()

        h_wait(s3)

        @pl.when(c == 1)
        def _():
            h_copy(s3, to_xp).start()
            h_copy(s3, to_xm).start()

    def step_c(d):
        zs = z_of(d)
        even = zs % 2 == 0
        s4 = slot_of(zs, (x + 2) % 4, yb)
        s5, s6 = slot_of(zs, xm, 1 - yb), slot_of(zs, xp, 1 - yb)
        h_wait(s4)

        @pl.when(c == 0)
        def _():
            h_copy(s4, to_yp).start()

        h_wait(s5)

        @pl.when((c == 1) & even)
        def _():
            h_copy(s5, to_xp).start()

        h_wait(s6)

        @pl.when((c == 1) & jnp.logical_not(even))
        def _():
            h_copy(s6, to_xm).start()

    def step_d(d):
        zs = z_of(d)
        h_wait(slot_of(zs, (x + 2) % 4, 1 - yb))

        @pl.loop(0, 2)
        def _(g):
            for k in range(4):
                stage[pl.ds(k * ROWS, ROWS), :] = raw[zs * 8 + g * 4 + k].astype(jnp.float32)
            row = pl.multiple_of(zs * GROUP + g * 4 * ROWS, 16)
            act[pl.ds(row, 4 * ROWS), :] = stage[...].astype(jnp.bfloat16)

    def w_direct(i):
        q, half = i // 2, i % 2
        for n in range(2):
            zs = jnp.where(half == 0, w_z(n), w_z(n + 2))
            w_wait(q, zs, 0)
            w_send(q, zs, 0, 1, to_ys)
            w_send(q, zs, 0, 0, to_core)

    def w_across(i):
        q, half = i // 2, i % 2
        for n in range(2):
            zs = jnp.where(half == 0, w_z(n), w_z(n + 2))
            w_wait(q, zs, 1)
            w_send(q, zs, 1, 1, to_core)

    step_a(jnp.int32(0))
    w_first(0)
    keep = pltpu.make_async_copy(lab_ref, labs.at[z], local_sem)
    keep.start()
    keep.wait()

    def lab_copy(k, zz):
        return pltpu.make_async_remote_copy(
            src_ref=lab_ref, dst_ref=labs.at[zz], send_sem=lsend, recv_sem=lrecv.at[zz],
            device_id=dev((z + k) % 8, y, x, c), device_id_type=pl.DeviceIdType.MESH)

    @pl.loop(1, 8)
    def _(k):
        lab_copy(k, z).start()

    @pl.loop(0, 11)
    def _(i):
        @pl.when((i % 2 == 0) & (i < 2 * NQ - 2))
        def _():
            w_first(i // 2 + 1)

        @pl.when((i >= 1) & (i < 8))
        def _():
            step_a(i)

        @pl.when((i >= 1) & (i < 9))
        def _():
            step_b(i - 1)

        @pl.when(i < 2 * NQ)
        def _():
            w_direct(i)

        @pl.when((i >= 2) & (i < 10))
        def _():
            step_c(i - 2)

        @pl.when(i >= 1)
        def _():
            w_across(i - 1)

        @pl.when(i >= 3)
        def _():
            step_d(i - 3)

    @pl.loop(1, 8)
    def _(k):
        zz = (z + k) % 8
        pltpu.make_async_copy(labs.at[zz], labs.at[zz], lrecv.at[zz]).wait()

    pltpu.make_async_copy(labs.at[pl.ds(0, 7)], labs.at[pl.ds(0, 7)], lsend).wait()

    @pl.loop(0, 8)
    def _(zz):
        line = jnp.broadcast_to(labs[zz][0:1, :], (128, 256))
        labcol[pl.ds(pl.multiple_of(zz * GROUP, 8), GROUP), :] = jnp.transpose(line)[:GROUP]

    m_ref[...] = jnp.full_like(m_ref, LEAST)
    s_ref[...] = jnp.zeros_like(s_ref)
    p_ref[...] = jnp.zeros_like(p_ref)
    lane = lax.broadcasted_iota(jnp.int32, (MT, 128), 1)

    @pl.loop(0, NQ)
    def _(q):
        @pl.loop(0, 4)
        def _(n):
            zs = (1 - c) + 2 * n
            w_wait(q, zs, 0)
            w_wait(q, zs, 1)

        @pl.loop(0, TOK // MT)
        def _(t):
            rows = pl.ds(pl.multiple_of(t * MT, MT), MT)
            logits = jnp.dot(act[rows, :], wbuf[q], preferred_element_type=jnp.float32)
            a, b = logits[:, :CH], logits[:, CH:]
            first = z * BLOCK + q * CH
            target = labcol[rows, :] - lane
            at_a = target == (y * 4 + x) * (8 * BLOCK) + first
            at_b = target == (ystar * 4 + x) * (8 * BLOCK) + first
            p_ref[rows, :] += jnp.where(at_a, a, 0.0) + jnp.where(at_b, b, 0.0)
            old = m_ref[rows, :]
            new = jnp.maximum(old, jnp.maximum(a, b))
            m_ref[rows, :] = new
            s_ref[rows, :] = s_ref[rows, :] * jnp.exp(old - new) + (jnp.exp(a - new) + jnp.exp(b - new))

    @pl.loop(0, 8)
    def _(zz):
        rows = pl.ds(pl.multiple_of(zz * GROUP, 8), GROUP)
        m = m_ref[rows, :]
        top = jnp.max(m, axis=1, keepdims=True)
        total = jnp.sum(s_ref[rows, :] * jnp.exp(m - top), axis=1, keepdims=True)
        got = jnp.sum(p_ref[rows, :], axis=1, keepdims=True)
        ids = lax.broadcasted_iota(jnp.int32, (GROUP, 128), 1)
        packed = jnp.where(ids == 0, top, jnp.where(ids == 1, total, got))
        packed = jnp.concatenate([packed, jnp.zeros((256 - GROUP, 128), jnp.float32)], axis=0)
        out_ref[zz] = jnp.transpose(packed)[:8]

    pltpu.make_async_copy(raw.at[pl.ds(0, 63)], raw.at[pl.ds(0, 63)], hsend).wait()

    @pl.when(selfish)
    def _():
        part = wbuf.at[:, pl.ds(0, D - 256), :]
        pltpu.make_async_copy(part, part, wsend).wait()

    @pl.when(jnp.logical_not(selfish))
    def _():
        pltpu.make_async_copy(wbuf, wbuf, wsend).wait()


def partial_stats(hidden, weight, labels):
    return pl.pallas_call(
        main_kernel,
        out_shape=jax.ShapeDtypeStruct((8, 8, 256), jnp.float32),
        in_specs=[
            pl.BlockSpec(memory_space=pl.ANY),
            pl.BlockSpec(memory_space=pl.ANY),
            pl.BlockSpec(memory_space=pltpu.VMEM),
        ],
        out_specs=pl.BlockSpec(memory_space=pltpu.VMEM),
        scratch_shapes=[
            pltpu.VMEM((SLOTS, ROWS, D), jnp.bfloat16),
            pltpu.VMEM((TOK, D), jnp.bfloat16),
            pltpu.VMEM((NQ, D, 2 * CH), jnp.bfloat16),
            pltpu.VMEM((8, 8, 256), jnp.int32),
            pltpu.VMEM((TOK, 128), jnp.int32),
            pltpu.VMEM((4 * ROWS, D), jnp.float32),
            pltpu.VMEM((TOK, 128), jnp.float32),
            pltpu.VMEM((TOK, 128), jnp.float32),
            pltpu.VMEM((TOK, 128), jnp.float32),
            pltpu.SemaphoreType.DMA((SLOTS,)),
            pltpu.SemaphoreType.DMA,
            pltpu.SemaphoreType.DMA((NQ, 8, 2)),
            pltpu.SemaphoreType.DMA,
            pltpu.SemaphoreType.DMA((8,)),
            pltpu.SemaphoreType.DMA,
            pltpu.SemaphoreType.DMA,
        ],
        compiler_params=pltpu.CompilerParams(
            collective_id=0, has_side_effects=True, vmem_limit_bytes=60 * 2**20),
        name="gather_and_score",
    )(hidden, weight, labels)


def from_everyone(x, axis):
    devices = lax.axis_size(axis)
    return lax.all_to_all(jnp.broadcast_to(x[None], (devices, *x.shape)), axis, 0, 0, tiled=True)


def merged(stats, axes):
    top = jnp.max(stats[..., 0, :], axis=axes, keepdims=True)
    total = jnp.sum(stats[..., 1, :] * jnp.exp(stats[..., 0, :] - top), axis=axes)
    return jnp.stack([jnp.squeeze(top, axes), total, jnp.sum(stats[..., 2, :], axis=axes)], axis=-2)


def shards(hidden, out_weight, labels, text_mask):
    v = lax.axis_index("vocab")
    core, pair = v % 2, v // 16
    mine = labels.reshape(2, 2, 4, 2, ROWS).transpose(0, 3, 2, 1, 4).reshape(4, GROUP)
    mine = lax.dynamic_slice_in_dim(mine, pair * 2 + core, 1, 0)
    mine = jnp.broadcast_to(jnp.pad(mine, ((0, 0), (0, 256 - GROUP))), (8, 256))
    stats = partial_stats(hidden, out_weight, mine)
    stats = lax.all_to_all(stats, "dp", 0, 0, tiled=True)[:, :3, :GROUP]
    stats = from_everyone(merged(stats, 0), "vocab")
    stats = merged(stats.reshape(2, 2, 4, 2, 3, GROUP), (1, 2))
    loss = stats[:, :, 0] + jnp.log(stats[:, :, 1]) - stats[:, :, 2]
    loss = loss.reshape(2, 2, 4, 2, ROWS).transpose(0, 3, 2, 1, 4).reshape(-1)
    weights_text = text_mask.astype(jnp.float32)
    token_loss = weights_text * loss
    sums = jnp.stack([jnp.sum(token_loss), jnp.sum(weights_text)])
    loss_sum, tally = from_everyone(sums, "dp").sum(axis=0)
    mean_loss = loss_sum / jnp.maximum(tally, jnp.float32(1.0))
    return (token_loss, mean_loss)


def solution(mesh):
    in_specs = (P(("dp", "vocab"), None), P("dp", "vocab"), P("dp"), P("dp"))
    out_specs = (P("dp"), P())
    return jax.shard_map(shards, mesh=mesh, in_specs=in_specs, out_specs=out_specs, check_vma=False)
```

```python
import functools

import jax
import jax.numpy as jnp
from jax import lax
from jax.experimental import pallas as pl
from jax.experimental.pallas import tpu as pltpu
from jax.sharding import PartitionSpec as P

ROWS = 20
D = 4096
KROWS = D // 8
BLOCK = 640
CH = 128
NQ = BLOCK // CH
GROUP = 8 * ROWS
TOK = 8 * GROUP
LEAST = float(jnp.finfo(jnp.float32).min)
MT = 320
RING = (8, 8, 18, 18, 27, 27, 42)
SPREAD = (8, 13, 20, 27, 34, 42, 50)
ROUND1 = (6, 14, 20, 28, 35, 43, 51, 58)
ROUND2 = (18, 25, 32, 38, 46, 53, 60, 66)
ROUND3 = (26, 34, 42, 49, 57, 63, 69, 75)
SEND = (0, 8, 18, 27, 32, 37, 43, 48, 53, 58)
DIRECT = (12, 20, 29, 37, 43, 48, 54, 60, 65, 71)
ACROSS = (21, 29, 38, 46, 52, 57, 63, 69, 74, 80)
OTHER = (31, 48, 59, 71, 82)
CELLS = ((0, 0, 40), (1, 0, 52), (0, 1, 52), (1, 1, 56), (0, 2, 60), (1, 2, 64), (2, 0, 64), (2, 1, 68), (2, 2, 68), (0, 3, 72), (1, 3, 72), (2, 3, 76), (3, 0, 76), (3, 1, 76), (3, 2, 77), (3, 3, 77))
STEP_US = 4
STEPS = 82 // STEP_US + 1
MESH = pl.DeviceIdType.MESH


def pick(n, values):
    out = jnp.int32(values[0])
    for k in range(1, len(values)):
        if values[k] != values[k - 1]:
            out = jnp.where(n >= k, jnp.int32(values[k]), out)
    return out


def joined(tiles):
    top = functools.reduce(jnp.maximum, [t[0:2] for t in tiles])
    total = functools.reduce(jnp.add, [t[2:4] * jnp.exp(t[0:2] - top) for t in tiles])
    got = functools.reduce(jnp.add, [t[4:6] for t in tiles])
    return top, total, got


def main_kernel(
    h_ref, w_ref, lab_ref, mask_ref, loss_ref, mean_ref,
    act, braw, wbuf, mine, perm, lab_out, mask_in, loss_in, labs, labcol, stage, m_ref, s_ref, p_ref,
    out1, in1, out2, in2, out3, in3,
    hrecv, hsend, wrecv, wsend, lrecv, lsend, local_sem, fsend, frecv,
):
    z = lax.axis_index("dp")
    v = lax.axis_index("vocab")
    c = v % 2
    x = (v // 2) % 4
    y = v // 8
    yb = y % 2
    xp, xm = (x + 1) % 4, (x + 3) % 4
    zp, zm = (z + 1) % 8, (z + 7) % 8
    ypair = y + 1 - 2 * yb
    ystar = (y + 2 * yb + 3) % 4

    def dev(zz, yy, xx, cc):
        return {"dp": zz, "vocab": (yy * 4 + xx) * 2 + cc}

    bar = pltpu.get_barrier_semaphore()

    def greet(d):
        pl.semaphore_signal(bar, inc=1, device_id=d, device_id_type=MESH)

    @pl.loop(1, 8)
    def _(k):
        greet(dev((z + k) % 8, y, x, c))
        greet(dev((z + k) % 8, y, x, 1 - c))

    @pl.loop(1, 32)
    def _(k):
        greet({"dp": z, "vocab": (v + k) % 32})

    def rows_of(d, piece):
        return pl.ds(pl.multiple_of(d * GROUP + piece * 16, 16), 16)

    own = x * 2 + yb
    first = pltpu.make_async_copy(h_ref.at[pl.ds(0, 16)], act.at[rows_of(0, own)], local_sem)
    first.start()
    second = pltpu.make_async_copy(h_ref, mine, lsend)
    second.start()
    second.wait()
    few = mine[...].astype(jnp.float32)[16:ROWS]
    for kq in range(4):
        stage[kq * 4 : kq * 4 + 4, 0 : D // 4] = few[:, kq * (D // 4) : (kq + 1) * (D // 4)]
    braw[own] = stage[:, 0 : D // 4].astype(jnp.bfloat16)
    first.wait()
    pl.semaphore_wait(bar, 45)

    def h_copy(d, piece, to_d, device):
        for src, dst in (
            (act.at[rows_of(d, piece)], act.at[rows_of(to_d, piece)]),
            (braw.at[d * 8 + piece], braw.at[to_d * 8 + piece]),
        ):
            pltpu.make_async_remote_copy(
                src_ref=src, dst_ref=dst, send_sem=hsend, recv_sem=hrecv.at[to_d * 8 + piece],
                device_id=device, device_id_type=MESH).start()

    def h_wait(d, piece):
        size = wbuf.at[0, pl.ds(0, 320), :]
        pltpu.make_async_copy(size, size, hrecv.at[d * 8 + piece]).wait()

    to_zp, to_zm = dev(zp, y, x, c), dev(zm, y, x, c)
    to_xp, to_xm = dev(z, y, xp, c), dev(z, y, xm, c)
    to_yp, to_ys = dev(z, ypair, x, c), dev(z, ystar, x, c)
    to_core = dev(z, y, x, 1 - c)

    def z_of(d):
        k = (d + 1) // 2
        return (z + jnp.where(d % 2 == 1, 8 - k, k)) % 8

    def w_at(q, zs, side):
        return wbuf.at[q, pl.ds(pl.multiple_of(zs * KROWS, KROWS), KROWS), pl.ds(side * CH, CH)]

    def w_wait(q, zs, side):
        pltpu.make_async_copy(w_at(q, zs, side), w_at(q, zs, side), wrecv.at[q, zs, side]).wait()

    def w_send(q, zs, side, to_side, d):
        pltpu.make_async_remote_copy(
            src_ref=w_at(q, zs, side), dst_ref=w_at(q, zs, to_side), send_sem=wsend,
            recv_sem=wrecv.at[q, zs, to_side], device_id=d, device_id_type=MESH).start()

    tcore = z % 2
    selfish = jnp.logical_and(z // 4 == c, tcore == c)

    def w_first(i):
        q, half = i // 2, i % 2

        def one(j):
            p = 4 * c + j
            src = w_ref.at[:, pl.ds(pl.multiple_of(j * BLOCK + q * CH, CH), CH)]
            mine = jnp.logical_and(p == z, tcore == c)

            @pl.when(mine)
            def _():
                pltpu.make_async_copy(src, w_at(q, z, 0), wrecv.at[q, z, 0]).start()

            @pl.when(jnp.logical_not(mine))
            def _():
                pltpu.make_async_remote_copy(
                    src_ref=src, dst_ref=w_at(q, z, 0), send_sem=wsend, recv_sem=wrecv.at[q, z, 0],
                    device_id=dev(p, y, x, tcore), device_id_type=MESH).start()

        @pl.loop(0, 4)
        def _(j):
            away = (4 * c + j - z + 8) % 8

            @pl.when(((away <= 2) | (away >= 6)) == (half == 0))
            def _():
                one(j)

    same = (c + z) % 2

    def w_z(n):
        a, b = ((0, 1), (2, 7), (6, 3), (4, 5))[n]
        return (z + jnp.where(same == 0, a, b)) % 8

    def x_first(zs):
        return (c == 0) & (zs != 7)

    def ring(d):
        @pl.when(d > 0)
        def _():
            h_wait(d, own)

        even = z_of(d) % 2 == 0
        odd_d = d % 2 == 1
        up = (d == 0) | (odd_d & (d <= 3)) | ((d == 5) & even)
        down = (d == 0) | (jnp.logical_not(odd_d) & (d <= 4)) | ((d == 6) & jnp.logical_not(even))

        @pl.when(up)
        def _():
            h_copy(d, own, jnp.where(d == 0, 1, d + 2), to_zp)

        @pl.when(down)
        def _():
            h_copy(d, own, jnp.where(d == 6, 7, d + 2), to_zm)

    def step_a(d):
        h_copy(d, own, d, to_xp)
        h_copy(d, own, d, to_xm)
        h_copy(d, own, d, to_yp)

    def step_b(d):
        zs = z_of(d)
        even = zs % 2 == 0
        xf = x_first(zs)
        s1, s2, s3 = xm * 2 + yb, xp * 2 + yb, x * 2 + 1 - yb
        h_wait(d, s1)

        @pl.when(even)
        def _():
            h_copy(d, s1, d, to_xp)

        @pl.when(xf)
        def _():
            h_copy(d, s1, d, to_yp)

        h_wait(d, s2)

        @pl.when(jnp.logical_not(even))
        def _():
            h_copy(d, s2, d, to_xm)

        @pl.when(xf)
        def _():
            h_copy(d, s2, d, to_yp)

        h_wait(d, s3)

        @pl.when(jnp.logical_not(xf))
        def _():
            h_copy(d, s3, d, to_xp)
            h_copy(d, s3, d, to_xm)

    def step_c(d):
        zs = z_of(d)
        even = zs % 2 == 0
        xf = x_first(zs)
        s4 = ((x + 2) % 4) * 2 + yb
        s5, s6 = xm * 2 + 1 - yb, xp * 2 + 1 - yb
        h_wait(d, s4)

        @pl.when(xf)
        def _():
            h_copy(d, s4, d, to_yp)

        h_wait(d, s5)

        @pl.when(jnp.logical_not(xf) & even)
        def _():
            h_copy(d, s5, d, to_xp)

        h_wait(d, s6)

        @pl.when(jnp.logical_not(xf) & jnp.logical_not(even))
        def _():
            h_copy(d, s6, d, to_xm)

    def step_d(d):
        h_wait(d, ((x + 2) % 4) * 2 + 1 - yb)

        @pl.loop(0, 2)
        def _(g):
            for k in range(4):
                piece = braw[d * 8 + g * 4 + k].astype(jnp.float32)
                for kq in range(4):
                    stage[pl.ds(k * 4, 4), pl.ds(kq * 1024, 1024)] = piece[kq * 4 : kq * 4 + 4]
            row = pl.multiple_of(d * GROUP + 128 + g * 16, 16)
            act[pl.ds(row, 16), :] = stage[...].astype(jnp.bfloat16)

    def w_direct(i):
        q, half = i // 2, i % 2
        for n in range(2):
            zs = jnp.where(half == 0, w_z(n), w_z(n + 2))
            w_wait(q, zs, 0)
            w_send(q, zs, 0, 1, to_ys)
            w_send(q, zs, 0, 0, to_core)

    def w_across(i):
        q, half = i // 2, i % 2
        for n in range(2):
            zs = jnp.where(half == 0, w_z(n), w_z(n + 2))
            w_wait(q, zs, 1)
            w_send(q, zs, 1, 1, to_core)

    def w_other(q):
        @pl.loop(0, 4)
        def _(n):
            zs = (1 - c) + 2 * n
            w_wait(q, zs, 0)
            w_wait(q, zs, 1)

    lane = lax.broadcasted_iota(jnp.int32, (MT, 128), 1)
    col_a = (y * 4 + x) * (8 * BLOCK) + z * BLOCK
    col_b = (ystar * 4 + x) * (8 * BLOCK) + z * BLOCK

    def cell(t, q):
        rows = pl.ds(pl.multiple_of(t * MT, MT), MT)
        logits = jnp.dot(act[rows, :], wbuf[q], preferred_element_type=jnp.float32)
        a, b = logits[:, :CH], logits[:, CH:]
        target = labcol[rows, :] - lane
        at_a = target == col_a + q * CH
        at_b = target == col_b + q * CH
        p_ref[rows, :] += jnp.where(at_a, a, 0.0) + jnp.where(at_b, b, 0.0)
        old = m_ref[rows, :]
        new = jnp.maximum(old, jnp.maximum(a, b))
        m_ref[rows, :] = new
        s_ref[rows, :] = s_ref[rows, :] * jnp.exp(old - new) + (jnp.exp(a - new) + jnp.exp(b - new))

    ring(jnp.int32(0))
    step_a(jnp.int32(0))

    def place(t):
        piece = (t * 3277) >> 16
        r = t - piece * ROWS
        s8 = ((piece >> 1) & 3) * 2 + ((piece >> 3) & 1)
        group = (piece >> 4) * 2 + (piece & 1)
        head = r < 16
        return jnp.where(head, s8 * 16 + r, s8 * 4 + r - 16), group * 2 + jnp.where(head, 0, 1)

    tile_row = lax.broadcasted_iota(jnp.int32, (8, 128), 0)
    tile_lane = lax.broadcasted_iota(jnp.int32, (8, 128), 1)

    def is_row(k):
        return place(k * 128 + tile_lane)[1] == tile_row

    for k in range(5):
        ids = lax.broadcasted_iota(jnp.int32, (128, 128), 0) + k * 128
        lanes = lax.broadcasted_iota(jnp.int32, (128, 128), 1)
        perm[k] = jnp.where(place(ids)[0] == lanes, 1.0, 0.0)

    def by_piece(ref):
        out = jnp.zeros((8, 128), jnp.float32)
        for k in range(5):
            line = jnp.broadcast_to(ref[k : k + 1].astype(jnp.float32), (8, 128))
            out += jnp.dot(
                jnp.where(is_row(k), line, 0.0), perm[k],
                preferred_element_type=jnp.float32, precision=lax.Precision.HIGHEST)
        return out

    mask_in[...] = by_piece(mask_ref)
    labels = by_piece(lab_ref)
    group = (y // 2) * 2 + c
    lines = [
        jnp.sum(jnp.where(tile_row == group * 2 + k, labels, 0.0), axis=0, keepdims=True) for k in range(2)
    ]
    lab_out[...] = jnp.where(tile_row == 0, lines[0], lines[1]).astype(jnp.int32)

    @pl.loop(1, 8)
    def _(k):
        pltpu.make_async_remote_copy(
            src_ref=lab_out, dst_ref=labs.at[z], send_sem=lsend, recv_sem=lrecv,
            device_id=dev((z + k) % 8, y, x, c), device_id_type=MESH).start()

    labs[z] = lab_out[...]
    m_ref[...] = jnp.full_like(m_ref, LEAST)
    s_ref[...] = jnp.zeros_like(s_ref)
    p_ref[...] = jnp.zeros_like(p_ref)

    def at_step(i, times, body):
        ready = [sum(1 for k in times if k // STEP_US < n) for n in range(STEPS + 1)]
        pl.loop(pick(i, ready[:-1]), pick(i, ready[1:]))(body)

    @pl.loop(0, STEPS)
    def _(i):
        at_step(i, RING, lambda n: ring(n + 1))
        at_step(i, SPREAD, lambda n: step_a(n + 1))
        at_step(i, SEND, w_first)
        at_step(i, ROUND1, step_b)
        at_step(i, DIRECT, w_direct)
        at_step(i, ROUND2, step_c)
        at_step(i, ACROSS, w_across)
        at_step(i, OTHER, w_other)

        @pl.when(i == 5)
        def _():
            seven = labs.at[pl.ds(0, 7)]
            pltpu.make_async_copy(seven, seven, lrecv).wait()
            pltpu.make_async_copy(seven, seven, lsend).wait()

            @pl.loop(0, 8)
            def _(d):
                pair = labs[z_of(d)]
                for k, size in ((0, 128), (1, 32)):
                    line = jnp.transpose(jnp.broadcast_to(pair[k : k + 1], (128, 128)))
                    labcol[pl.ds(pl.multiple_of(d * GROUP + k * 128, 32), size), :] = line[:size]

        at_step(
            i, [k[2] for k in CELLS],
            lambda n: cell(pick(n, [k[0] for k in CELLS]), pick(n, [k[1] for k in CELLS])))
        at_step(i, ROUND3, step_d)

    ids = lax.broadcasted_iota(jnp.int32, (128, 128), 1)

    def to_owner(d):
        columns = []
        for base, size in ((0, 128), (128, 32)):
            rows = pl.ds(pl.multiple_of(d * GROUP + base, 32), size)
            m = m_ref[rows, :]
            top = jnp.max(m, axis=1, keepdims=True)
            total = jnp.sum(s_ref[rows, :] * jnp.exp(m - top), axis=1, keepdims=True)
            got = jnp.sum(p_ref[rows, :], axis=1, keepdims=True)
            columns.append((top, total, got))
        packed = jnp.zeros((128, 128), jnp.float32)
        for k in range(3):
            packed = jnp.where(ids == 2 * k, columns[0][k], packed)
            fill = jnp.full((96, 1), 1.0 if k == 1 else 0.0, jnp.float32)
            packed = jnp.where(ids == 2 * k + 1, jnp.concatenate([columns[1][k], fill], axis=0), packed)
        out1[d] = jnp.transpose(packed)[:8]

        @pl.when(d > 0)
        def _():
            pltpu.make_async_remote_copy(
                src_ref=out1.at[d], dst_ref=in1.at[z], send_sem=fsend.at[0], recv_sem=frecv.at[0],
                device_id=dev(z_of(d), y, x, c), device_id_type=MESH).start()

    @pl.loop(0, 4)
    def _(k):
        t = 3 - k
        cell(t, NQ - 1)
        to_owner(2 * t + 1)
        to_owner(2 * t)

    in1[z] = out1[0]
    seven = in1.at[pl.ds(0, 7)]
    pltpu.make_async_copy(seven, seven, frecv.at[0]).wait()
    top, total, got = joined([in1[k] for k in range(8)])
    out2[0:2, :] = top
    out2[2:4, :] = total
    out2[4:6, :] = got
    out2[6:8, :] = got

    @pl.loop(1, 32)
    def _(k):
        pltpu.make_async_remote_copy(
            src_ref=out2, dst_ref=in2.at[v], send_sem=fsend.at[1], recv_sem=frecv.at[1],
            device_id={"dp": z, "vocab": (v + k) % 32}, device_id_type=MESH).start()

    in2[v] = out2[...]
    many = in2.at[pl.ds(0, 31)]
    pltpu.make_async_copy(many, many, frecv.at[1]).wait()
    for pair in range(2):
        for core in range(2):
            tiles = [in2[((pair * 2 + k // 4) * 4 + k % 4) * 2 + core] for k in range(8)]
            top, total, got = joined(tiles)
            at = (pair * 2 + core) * 2
            loss_in[at : at + 2, :] = mask_in[at : at + 2, :] * (top + jnp.log(total) - got)
    loss_sum = jnp.sum(loss_in[...], axis=(0, 1), keepdims=True)
    tally = jnp.sum(mask_in[...], axis=(0, 1), keepdims=True)
    out3[0:4, :] = jnp.broadcast_to(loss_sum, (4, 128))
    out3[4:8, :] = jnp.broadcast_to(tally, (4, 128))

    @pl.loop(1, 8)
    def _(k):
        pltpu.make_async_remote_copy(
            src_ref=out3, dst_ref=in3.at[z], send_sem=fsend.at[2], recv_sem=frecv.at[2],
            device_id=dev((z + k) % 8, y, x, c), device_id_type=MESH).start()

    in3[z] = out3[...]
    losses = loss_in[...]
    for k in range(5):
        moved = lax.dot_general(
            losses, perm[k], (((1,), (1,)), ((), ())),
            preferred_element_type=jnp.float32, precision=lax.Precision.HIGHEST)
        loss_ref[k : k + 1, :] = jnp.sum(jnp.where(is_row(k), moved, 0.0), axis=0, keepdims=True)
    seven3 = in3.at[pl.ds(0, 7)]
    pltpu.make_async_copy(seven3, seven3, frecv.at[2]).wait()
    sums = functools.reduce(jnp.add, [in3[k] for k in range(8)])
    mean_ref[...] = sums[0:1, 0:1] / jnp.maximum(sums[4:5, 0:1], 1.0)

    pltpu.make_async_copy(seven, seven, fsend.at[0]).wait()
    pltpu.make_async_copy(many, many, fsend.at[1]).wait()
    pltpu.make_async_copy(seven3, seven3, fsend.at[2]).wait()
    hidden_bytes = wbuf.at[:, pl.ds(0, 63 * 64), :]
    pltpu.make_async_copy(hidden_bytes, hidden_bytes, hsend).wait()

    @pl.when(selfish)
    def _():
        part = wbuf.at[:, pl.ds(0, D - 256), :]
        pltpu.make_async_copy(part, part, wsend).wait()

    @pl.when(jnp.logical_not(selfish))
    def _():
        pltpu.make_async_copy(wbuf, wbuf, wsend).wait()


def scored(hidden, weight, labels, mask):
    vmem = pl.BlockSpec(memory_space=pltpu.VMEM)
    anywhere = pl.BlockSpec(memory_space=pl.ANY)
    return pl.pallas_call(
        main_kernel,
        out_shape=(jax.ShapeDtypeStruct((5, 128), jnp.float32), jax.ShapeDtypeStruct((1, 1), jnp.float32)),
        in_specs=[anywhere, anywhere, vmem, vmem],
        out_specs=(vmem, vmem),
        scratch_shapes=[
            pltpu.VMEM((TOK, D), jnp.bfloat16),
            pltpu.VMEM((64, 16, D // 4), jnp.bfloat16),
            pltpu.VMEM((NQ, D, 2 * CH), jnp.bfloat16),
            pltpu.VMEM((ROWS, D), jnp.bfloat16),
            pltpu.VMEM((5, 128, 128), jnp.float32),
            pltpu.VMEM((8, 128), jnp.int32),
            pltpu.VMEM((8, 128), jnp.float32),
            pltpu.VMEM((8, 128), jnp.float32),
            pltpu.VMEM((8, 8, 128), jnp.int32),
            pltpu.VMEM((TOK, 128), jnp.int32),
            pltpu.VMEM((16, D), jnp.float32),
            pltpu.VMEM((TOK, 128), jnp.float32),
            pltpu.VMEM((TOK, 128), jnp.float32),
            pltpu.VMEM((TOK, 128), jnp.float32),
            pltpu.VMEM((8, 8, 128), jnp.float32),
            pltpu.VMEM((8, 8, 128), jnp.float32),
            pltpu.VMEM((8, 128), jnp.float32),
            pltpu.VMEM((32, 8, 128), jnp.float32),
            pltpu.VMEM((8, 128), jnp.float32),
            pltpu.VMEM((8, 8, 128), jnp.float32),
            pltpu.SemaphoreType.DMA((64,)),
            pltpu.SemaphoreType.DMA,
            pltpu.SemaphoreType.DMA((NQ, 8, 2)),
            pltpu.SemaphoreType.DMA,
            pltpu.SemaphoreType.DMA,
            pltpu.SemaphoreType.DMA,
            pltpu.SemaphoreType.DMA,
            pltpu.SemaphoreType.DMA((3,)),
            pltpu.SemaphoreType.DMA((3,)),
        ],
        compiler_params=pltpu.CompilerParams(
            collective_id=0, has_side_effects=True, vmem_limit_bytes=60 * 2**20),
        name="gather_and_score",
    )(hidden, weight, labels, mask)


def shards(hidden, out_weight, labels, text_mask):
    loss, mean = scored(hidden, out_weight, labels.reshape(5, 128), text_mask.reshape(5, 128))
    return (loss.reshape(-1), mean[0, 0])


def solution(mesh):
    in_specs = (P(("dp", "vocab"), None), P("dp", "vocab"), P("dp"), P("dp"))
    out_specs = (P("dp"), P())
    return jax.shard_map(shards, mesh=mesh, in_specs=in_specs, out_specs=out_specs, check_vma=False)
```

```python
import functools

import jax
import jax.numpy as jnp
from jax import lax
from jax.experimental import pallas as pl
from jax.experimental.pallas import tpu as pltpu
from jax.sharding import PartitionSpec as P

ROWS = 20
D = 4096
KROWS = D // 8
BLOCK = 640
CH = 128
NQ = BLOCK // CH
GROUP = 8 * ROWS
TOK = 8 * GROUP
LEAST = float(jnp.finfo(jnp.float32).min)
MT = 320
RING = (8, 8, 16, 16, 27, 27, 42)
SPREAD = (8, 13, 20, 27, 34, 42, 50)
ROUND1 = (6, 16, 20, 28, 35, 43, 51, 58)
ROUND2 = (18, 25, 32, 38, 46, 53, 60, 66)
ROUND3 = (26, 34, 42, 45, 53, 59, 66, 71)
SEND = (0, 8, 18, 27, 32, 37, 43, 48, 53, 58)
DIRECT = (12, 20, 29, 37, 43, 48, 54, 60, 65, 71)
ACROSS = (21, 29, 38, 46, 52, 57, 63, 69, 74, 80)
OTHER = (31, 52, 66, 74, 84)
CELLS = ((0, 0, 36), (1, 0, 48), (0, 1, 52), (1, 1, 56), (2, 0, 60), (2, 1, 64), (0, 2, 66), (1, 2, 67), (2, 2, 67), (3, 0, 74), (0, 3, 75), (1, 3, 75), (3, 1, 76), (2, 3, 76), (3, 2, 80), (3, 3, 80))
STEP_US = 4
STEPS = 84 // STEP_US + 1
MESH = pl.DeviceIdType.MESH


def pick(n, values):
    out = jnp.int32(values[0])
    for k in range(1, len(values)):
        if values[k] != values[k - 1]:
            out = jnp.where(n >= k, jnp.int32(values[k]), out)
    return out


def joined(tiles):
    top = functools.reduce(jnp.maximum, [t[0:2] for t in tiles])
    total = functools.reduce(jnp.add, [t[2:4] * jnp.exp(t[0:2] - top) for t in tiles])
    got = functools.reduce(jnp.add, [t[4:6] for t in tiles])
    return top, total, got


def main_kernel(
    h_ref, w_ref, lab_ref, mask_ref, loss_ref, mean_ref,
    act, braw, wbuf, mine, perm, lab_out, mask_in, loss_in, labs, labcol, stage, m_ref, s_ref, p_ref,
    out1, in1, out2, in2, out3, in3,
    hrecv, hsend, wrecv, wsend, lrecv, lsend, local_sem, fsend, frecv,
):
    z = lax.axis_index("dp")
    v = lax.axis_index("vocab")
    c = v % 2
    x = (v // 2) % 4
    y = v // 8
    yb = y % 2
    xp, xm = (x + 1) % 4, (x + 3) % 4
    zp, zm = (z + 1) % 8, (z + 7) % 8
    ypair = y + 1 - 2 * yb
    ystar = (y + 2 * yb + 3) % 4

    def dev(zz, yy, xx, cc):
        return {"dp": zz, "vocab": (yy * 4 + xx) * 2 + cc}

    bar = pltpu.get_barrier_semaphore()

    def greet(d):
        pl.semaphore_signal(bar, inc=1, device_id=d, device_id_type=MESH)

    @pl.loop(1, 8)
    def _(k):
        greet(dev((z + k) % 8, y, x, c))
        greet(dev((z + k) % 8, y, x, 1 - c))

    @pl.loop(1, 32)
    def _(k):
        greet({"dp": z, "vocab": (v + k) % 32})

    def rows_of(d, piece):
        return pl.ds(pl.multiple_of(d * GROUP + piece * 16, 16), 16)

    own = x * 2 + yb
    first = pltpu.make_async_copy(h_ref.at[pl.ds(0, 16)], act.at[rows_of(0, own)], local_sem)
    first.start()
    second = pltpu.make_async_copy(h_ref, mine, lsend)
    second.start()
    second.wait()
    few = mine[...].astype(jnp.float32)[16:ROWS]
    for kq in range(4):
        stage[kq * 4 : kq * 4 + 4, 0 : D // 4] = few[:, kq * (D // 4) : (kq + 1) * (D // 4)]
    braw[own] = stage[:, 0 : D // 4].astype(jnp.bfloat16)
    first.wait()
    pl.semaphore_wait(bar, 45)

    def h_copy(d, piece, to_d, device):
        for src, dst in (
            (act.at[rows_of(d, piece)], act.at[rows_of(to_d, piece)]),
            (braw.at[d * 8 + piece], braw.at[to_d * 8 + piece]),
        ):
            pltpu.make_async_remote_copy(
                src_ref=src, dst_ref=dst, send_sem=hsend, recv_sem=hrecv.at[to_d * 8 + piece],
                device_id=device, device_id_type=MESH).start()

    def h_wait(d, piece):
        size = wbuf.at[0, pl.ds(0, 320), :]
        pltpu.make_async_copy(size, size, hrecv.at[d * 8 + piece]).wait()

    to_zp, to_zm = dev(zp, y, x, c), dev(zm, y, x, c)
    to_xp, to_xm = dev(z, y, xp, c), dev(z, y, xm, c)
    to_yp, to_ys = dev(z, ypair, x, c), dev(z, ystar, x, c)
    to_core = dev(z, y, x, 1 - c)

    def z_of(d):
        k = (d + 1) // 2
        return (z + jnp.where(d % 2 == 1, 8 - k, k)) % 8

    def w_at(q, zs, side):
        return wbuf.at[q, pl.ds(pl.multiple_of(zs * KROWS, KROWS), KROWS), pl.ds(side * CH, CH)]

    def w_wait(q, zs, side):
        pltpu.make_async_copy(w_at(q, zs, side), w_at(q, zs, side), wrecv.at[q, zs, side]).wait()

    def w_send(q, zs, side, to_side, d):
        pltpu.make_async_remote_copy(
            src_ref=w_at(q, zs, side), dst_ref=w_at(q, zs, to_side), send_sem=wsend,
            recv_sem=wrecv.at[q, zs, to_side], device_id=d, device_id_type=MESH).start()

    tcore = z % 2
    selfish = jnp.logical_and(z // 4 == c, tcore == c)

    def w_first(i):
        q, half = i // 2, i % 2

        def one(j):
            p = 4 * c + j
            src = w_ref.at[:, pl.ds(pl.multiple_of(j * BLOCK + q * CH, CH), CH)]
            mine = jnp.logical_and(p == z, tcore == c)

            @pl.when(mine)
            def _():
                pltpu.make_async_copy(src, w_at(q, z, 0), wrecv.at[q, z, 0]).start()

            @pl.when(jnp.logical_not(mine))
            def _():
                pltpu.make_async_remote_copy(
                    src_ref=src, dst_ref=w_at(q, z, 0), send_sem=wsend, recv_sem=wrecv.at[q, z, 0],
                    device_id=dev(p, y, x, tcore), device_id_type=MESH).start()

        @pl.loop(0, 4)
        def _(j):
            away = (4 * c + j - z + 8) % 8

            @pl.when(((away <= 2) | (away >= 6)) == (half == 0))
            def _():
                one(j)

    same = (c + z) % 2

    def w_z(n):
        a, b = ((0, 1), (2, 7), (6, 3), (4, 5))[n]
        return (z + jnp.where(same == 0, a, b)) % 8

    def x_first(zs):
        return (c == 0) & (zs != 7)

    def ring(d):
        @pl.when(d > 0)
        def _():
            h_wait(d, own)

        even = z_of(d) % 2 == 0
        odd_d = d % 2 == 1
        up = (d == 0) | (odd_d & (d <= 3)) | ((d == 5) & even)
        down = (d == 0) | (jnp.logical_not(odd_d) & (d <= 4)) | ((d == 6) & jnp.logical_not(even))

        @pl.when(up)
        def _():
            h_copy(d, own, jnp.where(d == 0, 1, d + 2), to_zp)

        @pl.when(down)
        def _():
            h_copy(d, own, jnp.where(d == 6, 7, d + 2), to_zm)

    def step_a(d):
        h_copy(d, own, d, to_xp)
        h_copy(d, own, d, to_xm)
        h_copy(d, own, d, to_yp)

    def step_b(d):
        zs = z_of(d)
        even = zs % 2 == 0
        xf = x_first(zs)
        s1, s2, s3 = xm * 2 + yb, xp * 2 + yb, x * 2 + 1 - yb
        h_wait(d, s1)

        @pl.when(even)
        def _():
            h_copy(d, s1, d, to_xp)

        @pl.when(xf)
        def _():
            h_copy(d, s1, d, to_yp)

        h_wait(d, s2)

        @pl.when(jnp.logical_not(even))
        def _():
            h_copy(d, s2, d, to_xm)

        @pl.when(xf)
        def _():
            h_copy(d, s2, d, to_yp)

        h_wait(d, s3)

        @pl.when(jnp.logical_not(xf))
        def _():
            h_copy(d, s3, d, to_xp)
            h_copy(d, s3, d, to_xm)

    def step_c(d):
        zs = z_of(d)
        even = zs % 2 == 0
        xf = x_first(zs)
        s4 = ((x + 2) % 4) * 2 + yb
        s5, s6 = xm * 2 + 1 - yb, xp * 2 + 1 - yb
        h_wait(d, s4)

        @pl.when(xf)
        def _():
            h_copy(d, s4, d, to_yp)

        h_wait(d, s5)

        @pl.when(jnp.logical_not(xf) & even)
        def _():
            h_copy(d, s5, d, to_xp)

        h_wait(d, s6)

        @pl.when(jnp.logical_not(xf) & jnp.logical_not(even))
        def _():
            h_copy(d, s6, d, to_xm)

    def step_d(d):
        h_wait(d, ((x + 2) % 4) * 2 + 1 - yb)

        @pl.loop(0, 2)
        def _(g):
            for k in range(4):
                piece = braw[d * 8 + g * 4 + k].astype(jnp.float32)
                for kq in range(4):
                    stage[pl.ds(k * 4, 4), pl.ds(kq * 1024, 1024)] = piece[kq * 4 : kq * 4 + 4]
            row = pl.multiple_of(d * GROUP + 128 + g * 16, 16)
            act[pl.ds(row, 16), :] = stage[...].astype(jnp.bfloat16)

    def w_direct(i):
        q, half = i // 2, i % 2
        for n in range(2):
            zs = jnp.where(half == 0, w_z(n), w_z(n + 2))
            w_wait(q, zs, 0)
            w_send(q, zs, 0, 1, to_ys)
            w_send(q, zs, 0, 0, to_core)

    def w_across(i):
        q, half = i // 2, i % 2
        for n in range(2):
            zs = jnp.where(half == 0, w_z(n), w_z(n + 2))
            w_wait(q, zs, 1)
            w_send(q, zs, 1, 1, to_core)

    def w_other(q):
        @pl.loop(0, 4)
        def _(n):
            zs = (1 - c) + 2 * n
            w_wait(q, zs, 0)
            w_wait(q, zs, 1)

    lane = lax.broadcasted_iota(jnp.int32, (MT, 128), 1)
    col_a = (y * 4 + x) * (8 * BLOCK) + z * BLOCK
    col_b = (ystar * 4 + x) * (8 * BLOCK) + z * BLOCK

    def cell(t, q):
        rows = pl.ds(t * MT if isinstance(t, int) else pl.multiple_of(t * MT, MT), MT)
        logits = jnp.dot(act[rows, :], wbuf[q], preferred_element_type=jnp.float32)
        a, b = logits[:, :CH], logits[:, CH:]
        target = labcol[rows, :] - lane
        at_a = target == col_a + q * CH
        at_b = target == col_b + q * CH
        p_ref[rows, :] += jnp.where(at_a, a, 0.0) + jnp.where(at_b, b, 0.0)
        old = m_ref[rows, :]
        new = jnp.maximum(old, jnp.maximum(a, b))
        m_ref[rows, :] = new
        s_ref[rows, :] = s_ref[rows, :] * jnp.exp(old - new) + (jnp.exp(a - new) + jnp.exp(b - new))

    ring(jnp.int32(0))
    step_a(jnp.int32(0))

    def place(t):
        piece = (t * 3277) >> 16
        r = t - piece * ROWS
        s8 = ((piece >> 1) & 3) * 2 + ((piece >> 3) & 1)
        group = (piece >> 4) * 2 + (piece & 1)
        head = r < 16
        return jnp.where(head, s8 * 16 + r, s8 * 4 + r - 16), group * 2 + jnp.where(head, 0, 1)

    tile_row = lax.broadcasted_iota(jnp.int32, (8, 128), 0)
    tile_lane = lax.broadcasted_iota(jnp.int32, (8, 128), 1)

    def is_row(k):
        return place(k * 128 + tile_lane)[1] == tile_row

    for k in range(5):
        ids = lax.broadcasted_iota(jnp.int32, (128, 128), 0) + k * 128
        lanes = lax.broadcasted_iota(jnp.int32, (128, 128), 1)
        perm[k] = jnp.where(place(ids)[0] == lanes, 1.0, 0.0)

    def by_piece(ref):
        out = jnp.zeros((8, 128), jnp.float32)
        for k in range(5):
            line = jnp.broadcast_to(ref[k : k + 1].astype(jnp.float32), (8, 128))
            out += jnp.dot(
                jnp.where(is_row(k), line, 0.0), perm[k],
                preferred_element_type=jnp.float32, precision=lax.Precision.HIGHEST)
        return out

    mask_in[...] = by_piece(mask_ref)
    labels = by_piece(lab_ref)
    group = (y // 2) * 2 + c
    lines = [
        jnp.sum(jnp.where(tile_row == group * 2 + k, labels, 0.0), axis=0, keepdims=True) for k in range(2)
    ]
    lab_out[...] = jnp.where(tile_row == 0, lines[0], lines[1]).astype(jnp.int32)

    @pl.loop(1, 8)
    def _(k):
        pltpu.make_async_remote_copy(
            src_ref=lab_out, dst_ref=labs.at[z], send_sem=lsend, recv_sem=lrecv,
            device_id=dev((z + k) % 8, y, x, c), device_id_type=MESH).start()

    labs[z] = lab_out[...]
    m_ref[...] = jnp.full_like(m_ref, LEAST)
    s_ref[...] = jnp.zeros_like(s_ref)
    p_ref[...] = jnp.zeros_like(p_ref)

    def at_step(i, times, body):
        ready = [sum(1 for k in times if k // STEP_US < n) for n in range(STEPS + 1)]
        pl.loop(pick(i, ready[:-1]), pick(i, ready[1:]))(body)

    @pl.loop(0, STEPS)
    def _(i):
        at_step(i, RING, lambda n: ring(n + 1))
        at_step(i, SPREAD, lambda n: step_a(n + 1))
        at_step(i, SEND, w_first)
        at_step(i, ROUND1, step_b)
        at_step(i, DIRECT, w_direct)
        at_step(i, ROUND2, step_c)
        at_step(i, ACROSS, w_across)
        at_step(i, OTHER, w_other)

        @pl.when(i == 5)
        def _():
            seven = labs.at[pl.ds(0, 7)]
            pltpu.make_async_copy(seven, seven, lrecv).wait()
            pltpu.make_async_copy(seven, seven, lsend).wait()

            @pl.loop(0, 8)
            def _(d):
                pair = labs[z_of(d)]
                for k, size in ((0, 128), (1, 32)):
                    line = jnp.transpose(jnp.broadcast_to(pair[k : k + 1], (128, 128)))
                    labcol[pl.ds(pl.multiple_of(d * GROUP + k * 128, 32), size), :] = line[:size]

        at_step(
            i, [k[2] for k in CELLS],
            lambda n: cell(pick(n, [k[0] for k in CELLS]), pick(n, [k[1] for k in CELLS])))
        at_step(i, ROUND3, step_d)

    ids = lax.broadcasted_iota(jnp.int32, (128, 128), 1)

    def pack(d):
        columns = []
        for base, size in ((0, 128), (128, 32)):
            rows = pl.ds(d * GROUP + base, size)
            m = m_ref[rows, :]
            top = jnp.max(m, axis=1, keepdims=True)
            total = jnp.sum(s_ref[rows, :] * jnp.exp(m - top), axis=1, keepdims=True)
            got = jnp.sum(p_ref[rows, :], axis=1, keepdims=True)
            columns.append((top, total, got))
        packed = jnp.zeros((128, 128), jnp.float32)
        for k in range(3):
            packed = jnp.where(ids == 2 * k, columns[0][k], packed)
            fill = jnp.full((96, 1), 1.0 if k == 1 else 0.0, jnp.float32)
            packed = jnp.where(ids == 2 * k + 1, jnp.concatenate([columns[1][k], fill], axis=0), packed)
        out1[d] = jnp.transpose(packed)[:8]

    def to_owner(d):
        pltpu.make_async_remote_copy(
            src_ref=out1.at[d], dst_ref=in1.at[z], send_sem=fsend.at[0], recv_sem=frecv.at[0],
            device_id=dev(z_of(d), y, x, c), device_id_type=MESH).start()

    for k in range(5):
        if k < 4:
            cell(3 - k, NQ - 1)
        if k > 0:
            for d in (9 - 2 * k, 8 - 2 * k):
                pack(d)
            for d in (9 - 2 * k, 8 - 2 * k):
                if d > 0:
                    to_owner(d)

    in1[z] = out1[0]
    seven = in1.at[pl.ds(0, 7)]
    pltpu.make_async_copy(seven, seven, frecv.at[0]).wait()
    top, total, got = joined([in1[k] for k in range(8)])
    out2[0:2, :] = top
    out2[2:4, :] = total
    out2[4:6, :] = got
    out2[6:8, :] = got

    @pl.loop(20, 51)
    def _(k):
        pltpu.make_async_remote_copy(
            src_ref=out2, dst_ref=in2.at[v], send_sem=fsend.at[1], recv_sem=frecv.at[1],
            device_id={"dp": z, "vocab": (v + k + k // 32) % 32}, device_id_type=MESH).start()

    in2[v] = out2[...]
    many = in2.at[pl.ds(0, 31)]
    pltpu.make_async_copy(many, many, frecv.at[1]).wait()
    for pair in range(2):
        for core in range(2):
            tiles = [in2[((pair * 2 + k // 4) * 4 + k % 4) * 2 + core] for k in range(8)]
            top, total, got = joined(tiles)
            at = (pair * 2 + core) * 2
            loss_in[at : at + 2, :] = top + jnp.log(total) - got
    loss_sum = jnp.sum(mask_in[...] * loss_in[...], axis=(0, 1), keepdims=True)
    tally = jnp.sum(mask_in[...], axis=(0, 1), keepdims=True)
    out3[0:4, :] = jnp.broadcast_to(loss_sum, (4, 128))
    out3[4:8, :] = jnp.broadcast_to(tally, (4, 128))

    for k in (4, 3, 5, 2, 6, 1, 7):
        pltpu.make_async_remote_copy(
            src_ref=out3, dst_ref=in3.at[z], send_sem=fsend.at[2], recv_sem=frecv.at[2],
            device_id=dev((z + k) % 8, y, x, c), device_id_type=MESH).start()

    in3[z] = out3[...]
    losses = loss_in[...]
    for k in range(5):
        moved = lax.dot_general(
            losses, perm[k], (((1,), (1,)), ((), ())),
            preferred_element_type=jnp.float32, precision=lax.Precision.HIGHEST)
        loss_ref[k : k + 1, :] = jnp.sum(jnp.where(is_row(k), moved, 0.0), axis=0, keepdims=True)
    seven3 = in3.at[pl.ds(0, 7)]
    pltpu.make_async_copy(seven3, seven3, frecv.at[2]).wait()
    sums = functools.reduce(jnp.add, [in3[k] for k in range(8)])
    mean_ref[...] = sums[0:1, 0:1] / jnp.maximum(sums[4:5, 0:1], 1.0)

    pltpu.make_async_copy(seven, seven, fsend.at[0]).wait()
    pltpu.make_async_copy(many, many, fsend.at[1]).wait()
    pltpu.make_async_copy(seven3, seven3, fsend.at[2]).wait()
    hidden_bytes = wbuf.at[:, pl.ds(0, 63 * 64), :]
    pltpu.make_async_copy(hidden_bytes, hidden_bytes, hsend).wait()

    @pl.when(selfish)
    def _():
        part = wbuf.at[:, pl.ds(0, D - 256), :]
        pltpu.make_async_copy(part, part, wsend).wait()

    @pl.when(jnp.logical_not(selfish))
    def _():
        pltpu.make_async_copy(wbuf, wbuf, wsend).wait()


def scored(hidden, weight, labels, mask):
    vmem = pl.BlockSpec(memory_space=pltpu.VMEM)
    anywhere = pl.BlockSpec(memory_space=pl.ANY)
    return pl.pallas_call(
        main_kernel,
        out_shape=(jax.ShapeDtypeStruct((5, 128), jnp.float32), jax.ShapeDtypeStruct((1, 1), jnp.float32)),
        in_specs=[anywhere, anywhere, vmem, vmem],
        out_specs=(vmem, vmem),
        scratch_shapes=[
            pltpu.VMEM((TOK, D), jnp.bfloat16),
            pltpu.VMEM((64, 16, D // 4), jnp.bfloat16),
            pltpu.VMEM((NQ, D, 2 * CH), jnp.bfloat16),
            pltpu.VMEM((ROWS, D), jnp.bfloat16),
            pltpu.VMEM((5, 128, 128), jnp.float32),
            pltpu.VMEM((8, 128), jnp.int32),
            pltpu.VMEM((8, 128), jnp.float32),
            pltpu.VMEM((8, 128), jnp.float32),
            pltpu.VMEM((8, 8, 128), jnp.int32),
            pltpu.VMEM((TOK, 128), jnp.int32),
            pltpu.VMEM((16, D), jnp.float32),
            pltpu.VMEM((TOK, 128), jnp.float32),
            pltpu.VMEM((TOK, 128), jnp.float32),
            pltpu.VMEM((TOK, 128), jnp.float32),
            pltpu.VMEM((8, 8, 128), jnp.float32),
            pltpu.VMEM((8, 8, 128), jnp.float32),
            pltpu.VMEM((8, 128), jnp.float32),
            pltpu.VMEM((32, 8, 128), jnp.float32),
            pltpu.VMEM((8, 128), jnp.float32),
            pltpu.VMEM((8, 8, 128), jnp.float32),
            pltpu.SemaphoreType.DMA((64,)),
            pltpu.SemaphoreType.DMA,
            pltpu.SemaphoreType.DMA((NQ, 8, 2)),
            pltpu.SemaphoreType.DMA,
            pltpu.SemaphoreType.DMA,
            pltpu.SemaphoreType.DMA,
            pltpu.SemaphoreType.DMA,
            pltpu.SemaphoreType.DMA((3,)),
            pltpu.SemaphoreType.DMA((3,)),
        ],
        compiler_params=pltpu.CompilerParams(
            collective_id=0, has_side_effects=True, vmem_limit_bytes=60 * 2**20),
        name="gather_and_score",
    )(hidden, weight, labels, mask)


def shards(hidden, out_weight, labels, text_mask):
    loss, mean = scored(hidden, out_weight, labels.reshape(5, 128), text_mask.reshape(5, 128))
    return (text_mask.astype(jnp.float32) * loss.reshape(-1), mean[0, 0])


def solution(mesh):
    in_specs = (P(("dp", "vocab"), None), P("dp", "vocab"), P("dp"), P("dp"))
    out_specs = (P("dp"), P())
    return jax.shard_map(shards, mesh=mesh, in_specs=in_specs, out_specs=out_specs, check_vma=False)
```

```python
import functools

import jax
import jax.numpy as jnp
from jax import lax
from jax.experimental import pallas as pl
from jax.experimental.pallas import tpu as pltpu
from jax.sharding import PartitionSpec as P

ROWS = 20
D = 4096
KROWS = D // 8
BLOCK = 640
CH = 128
NQ = BLOCK // CH
GROUP = 8 * ROWS
TOK = 8 * GROUP
LEAST = float(jnp.finfo(jnp.float32).min)
MT = 320
RING = (8, 8, 16, 16, 27, 27, 42)
SPREAD = (8, 13, 20, 27, 34, 42, 50)
ROUND1 = (6, 16, 20, 28, 35, 43, 51, 58)
ROUND2 = (18, 25, 32, 38, 46, 53, 60, 66)
ROUND3 = (26, 34, 42, 45, 53, 59, 66, 71)
SEND = (0, 8, 18, 27, 32, 37, 43, 48, 53, 58)
DIRECT = (12, 20, 29, 37, 43, 48, 54, 60, 65, 71)
ACROSS = (21, 29, 38, 46, 52, 57, 63, 69, 74, 80)
OTHER = (31, 52, 66, 74, 84)
CELLS = ((0, 0, 36), (1, 0, 48), (0, 1, 52), (1, 1, 56), (2, 0, 60), (2, 1, 64), (0, 2, 66), (1, 2, 67), (2, 2, 67), (3, 0, 74), (0, 3, 75), (1, 3, 75), (3, 1, 76), (2, 3, 76), (3, 2, 80), (3, 3, 80))
STEP_US = 4
STEPS = 84 // STEP_US + 1
MESH = pl.DeviceIdType.MESH


def pick(n, values):
    out = jnp.int32(values[0])
    for k in range(1, len(values)):
        if values[k] != values[k - 1]:
            out = jnp.where(n >= k, jnp.int32(values[k]), out)
    return out


def joined(tiles):
    top = functools.reduce(jnp.maximum, [t[0:2] for t in tiles])
    total = functools.reduce(jnp.add, [t[2:4] * jnp.exp(t[0:2] - top) for t in tiles])
    got = functools.reduce(jnp.add, [t[4:6] for t in tiles])
    return top, total, got


def main_kernel(
    h_ref, w_ref, lab_ref, mask_ref, loss_ref, mean_ref,
    act, braw, wbuf, mine, perm, lab_out, mask_in, loss_in, labs, labcol, stage, m_ref, s_ref, p_ref,
    out1, in1, out2, in2, out3, in3,
    hrecv, hsend, wrecv, wsend, lrecv, lsend, local_sem, fsend, frecv,
):
    z = lax.axis_index("dp")
    v = lax.axis_index("vocab")
    c = v % 2
    x = (v // 2) % 4
    y = v // 8
    yb = y % 2
    xp, xm = (x + 1) % 4, (x + 3) % 4
    zp, zm = (z + 1) % 8, (z + 7) % 8
    ypair = y + 1 - 2 * yb
    ystar = (y + 2 * yb + 3) % 4

    def dev(zz, yy, xx, cc):
        return {"dp": zz, "vocab": (yy * 4 + xx) * 2 + cc}

    bar = pltpu.get_barrier_semaphore()

    def greet(d):
        pl.semaphore_signal(bar, inc=1, device_id=d, device_id_type=MESH)

    @pl.loop(1, 8)
    def _(k):
        greet(dev((z + k) % 8, y, x, c))
        greet(dev((z + k) % 8, y, x, 1 - c))

    @pl.loop(1, 32)
    def _(k):
        greet({"dp": z, "vocab": (v + k) % 32})

    def rows_of(d, piece):
        return pl.ds(pl.multiple_of(d * GROUP + piece * 16, 16), 16)

    own = x * 2 + yb
    first = pltpu.make_async_copy(h_ref.at[pl.ds(0, 16)], act.at[rows_of(0, own)], local_sem)
    first.start()
    second = pltpu.make_async_copy(h_ref, mine, lsend)
    second.start()
    second.wait()
    few = mine[...].astype(jnp.float32)[16:ROWS]
    for kq in range(4):
        stage[kq * 4 : kq * 4 + 4, 0 : D // 4] = few[:, kq * (D // 4) : (kq + 1) * (D // 4)]
    braw[own] = stage[:, 0 : D // 4].astype(jnp.bfloat16)
    first.wait()

    def place(t):
        piece = (t * 3277) >> 16
        r = t - piece * ROWS
        s8 = ((piece >> 1) & 3) * 2 + ((piece >> 3) & 1)
        group = (piece >> 4) * 2 + (piece & 1)
        head = r < 16
        return jnp.where(head, s8 * 16 + r, s8 * 4 + r - 16), group * 2 + jnp.where(head, 0, 1)

    tile_row = lax.broadcasted_iota(jnp.int32, (8, 128), 0)
    tile_lane = lax.broadcasted_iota(jnp.int32, (8, 128), 1)

    def is_row(k):
        return place(k * 128 + tile_lane)[1] == tile_row

    for k in range(5):
        ids = lax.broadcasted_iota(jnp.int32, (128, 128), 0) + k * 128
        lanes = lax.broadcasted_iota(jnp.int32, (128, 128), 1)
        perm[k] = jnp.where(place(ids)[0] == lanes, 1.0, 0.0)

    def by_piece(ref):
        out = jnp.zeros((8, 128), jnp.float32)
        for k in range(5):
            line = jnp.broadcast_to(ref[k : k + 1].astype(jnp.float32), (8, 128))
            out += jnp.dot(
                jnp.where(is_row(k), line, 0.0), perm[k],
                preferred_element_type=jnp.float32, precision=lax.Precision.HIGHEST)
        return out

    mask_in[...] = by_piece(mask_ref)
    labels = by_piece(lab_ref)
    group = (y // 2) * 2 + c
    lines = [
        jnp.sum(jnp.where(tile_row == group * 2 + k, labels, 0.0), axis=0, keepdims=True) for k in range(2)
    ]
    lab_out[...] = jnp.where(tile_row == 0, lines[0], lines[1]).astype(jnp.int32)
    m_ref[...] = jnp.full_like(m_ref, LEAST)
    s_ref[...] = jnp.zeros_like(s_ref)
    p_ref[...] = jnp.zeros_like(p_ref)
    pl.semaphore_wait(bar, 45)

    def h_copy(d, piece, to_d, device):
        for src, dst in (
            (act.at[rows_of(d, piece)], act.at[rows_of(to_d, piece)]),
            (braw.at[d * 8 + piece], braw.at[to_d * 8 + piece]),
        ):
            pltpu.make_async_remote_copy(
                src_ref=src, dst_ref=dst, send_sem=hsend, recv_sem=hrecv.at[to_d * 8 + piece],
                device_id=device, device_id_type=MESH).start()

    def h_wait(d, piece):
        size = wbuf.at[0, pl.ds(0, 320), :]
        pltpu.make_async_copy(size, size, hrecv.at[d * 8 + piece]).wait()

    to_zp, to_zm = dev(zp, y, x, c), dev(zm, y, x, c)
    to_xp, to_xm = dev(z, y, xp, c), dev(z, y, xm, c)
    to_yp, to_ys = dev(z, ypair, x, c), dev(z, ystar, x, c)
    to_core = dev(z, y, x, 1 - c)

    def z_of(d):
        k = (d + 1) // 2
        return (z + jnp.where(d % 2 == 1, 8 - k, k)) % 8

    def w_at(q, zs, side):
        return wbuf.at[q, pl.ds(pl.multiple_of(zs * KROWS, KROWS), KROWS), pl.ds(side * CH, CH)]

    def w_wait(q, zs, side):
        pltpu.make_async_copy(w_at(q, zs, side), w_at(q, zs, side), wrecv.at[q, zs, side]).wait()

    def w_send(q, zs, side, to_side, d):
        pltpu.make_async_remote_copy(
            src_ref=w_at(q, zs, side), dst_ref=w_at(q, zs, to_side), send_sem=wsend,
            recv_sem=wrecv.at[q, zs, to_side], device_id=d, device_id_type=MESH).start()

    tcore = z % 2
    selfish = jnp.logical_and(z // 4 == c, tcore == c)

    def w_first(i):
        q, half = i // 2, i % 2

        def one(j):
            p = 4 * c + j
            src = w_ref.at[:, pl.ds(pl.multiple_of(j * BLOCK + q * CH, CH), CH)]
            mine = jnp.logical_and(p == z, tcore == c)

            @pl.when(mine)
            def _():
                pltpu.make_async_copy(src, w_at(q, z, 0), wrecv.at[q, z, 0]).start()

            @pl.when(jnp.logical_not(mine))
            def _():
                pltpu.make_async_remote_copy(
                    src_ref=src, dst_ref=w_at(q, z, 0), send_sem=wsend, recv_sem=wrecv.at[q, z, 0],
                    device_id=dev(p, y, x, tcore), device_id_type=MESH).start()

        @pl.loop(0, 4)
        def _(j):
            away = (4 * c + j - z + 8) % 8

            @pl.when(((away <= 2) | (away >= 6)) == (half == 0))
            def _():
                one(j)

    same = (c + z) % 2

    def w_z(n):
        a, b = ((0, 1), (2, 7), (6, 3), (4, 5))[n]
        return (z + jnp.where(same == 0, a, b)) % 8

    def x_first(zs):
        return (c == 0) & (zs != 7)

    def ring(d):
        @pl.when(d > 0)
        def _():
            h_wait(d, own)

        even = z_of(d) % 2 == 0
        odd_d = d % 2 == 1
        up = (d == 0) | (odd_d & (d <= 3)) | ((d == 5) & even)
        down = (d == 0) | (jnp.logical_not(odd_d) & (d <= 4)) | ((d == 6) & jnp.logical_not(even))

        @pl.when(up)
        def _():
            h_copy(d, own, jnp.where(d == 0, 1, d + 2), to_zp)

        @pl.when(down)
        def _():
            h_copy(d, own, jnp.where(d == 6, 7, d + 2), to_zm)

    def step_a(d):
        h_copy(d, own, d, to_xp)
        h_copy(d, own, d, to_xm)
        h_copy(d, own, d, to_yp)

    def step_b(d):
        zs = z_of(d)
        even = zs % 2 == 0
        xf = x_first(zs)
        s1, s2, s3 = xm * 2 + yb, xp * 2 + yb, x * 2 + 1 - yb
        h_wait(d, s1)

        @pl.when(even)
        def _():
            h_copy(d, s1, d, to_xp)

        @pl.when(xf)
        def _():
            h_copy(d, s1, d, to_yp)

        h_wait(d, s2)

        @pl.when(jnp.logical_not(even))
        def _():
            h_copy(d, s2, d, to_xm)

        @pl.when(xf)
        def _():
            h_copy(d, s2, d, to_yp)

        h_wait(d, s3)

        @pl.when(jnp.logical_not(xf))
        def _():
            h_copy(d, s3, d, to_xp)
            h_copy(d, s3, d, to_xm)

    def step_c(d):
        zs = z_of(d)
        even = zs % 2 == 0
        xf = x_first(zs)
        s4 = ((x + 2) % 4) * 2 + yb
        s5, s6 = xm * 2 + 1 - yb, xp * 2 + 1 - yb
        h_wait(d, s4)

        @pl.when(xf)
        def _():
            h_copy(d, s4, d, to_yp)

        h_wait(d, s5)

        @pl.when(jnp.logical_not(xf) & even)
        def _():
            h_copy(d, s5, d, to_xp)

        h_wait(d, s6)

        @pl.when(jnp.logical_not(xf) & jnp.logical_not(even))
        def _():
            h_copy(d, s6, d, to_xm)

    def step_d(d):
        h_wait(d, ((x + 2) % 4) * 2 + 1 - yb)

        @pl.loop(0, 2)
        def _(g):
            for k in range(4):
                piece = braw[d * 8 + g * 4 + k].astype(jnp.float32)
                for kq in range(4):
                    stage[pl.ds(k * 4, 4), pl.ds(kq * 1024, 1024)] = piece[kq * 4 : kq * 4 + 4]
            row = pl.multiple_of(d * GROUP + 128 + g * 16, 16)
            act[pl.ds(row, 16), :] = stage[...].astype(jnp.bfloat16)

    def w_direct(i):
        q, half = i // 2, i % 2
        for n in range(2):
            zs = jnp.where(half == 0, w_z(n), w_z(n + 2))
            w_wait(q, zs, 0)
            w_send(q, zs, 0, 1, to_ys)
            w_send(q, zs, 0, 0, to_core)

    def w_across(i):
        q, half = i // 2, i % 2
        for n in range(2):
            zs = jnp.where(half == 0, w_z(n), w_z(n + 2))
            w_wait(q, zs, 1)
            w_send(q, zs, 1, 1, to_core)

    def w_other(q):
        @pl.loop(0, 4)
        def _(n):
            zs = (1 - c) + 2 * n
            w_wait(q, zs, 0)
            w_wait(q, zs, 1)

    lane = lax.broadcasted_iota(jnp.int32, (MT, 128), 1)
    col_a = (y * 4 + x) * (8 * BLOCK) + z * BLOCK
    col_b = (ystar * 4 + x) * (8 * BLOCK) + z * BLOCK

    def cell(t, q):
        rows = pl.ds(t * MT if isinstance(t, int) else pl.multiple_of(t * MT, MT), MT)
        logits = jnp.dot(act[rows, :], wbuf[q], preferred_element_type=jnp.float32)
        a, b = logits[:, :CH], logits[:, CH:]
        target = labcol[rows, :] - lane
        at_a = target == col_a + q * CH
        at_b = target == col_b + q * CH
        p_ref[rows, :] += jnp.where(at_a, a, 0.0) + jnp.where(at_b, b, 0.0)
        old = m_ref[rows, :]
        new = jnp.maximum(old, jnp.maximum(a, b))
        m_ref[rows, :] = new
        s_ref[rows, :] = s_ref[rows, :] * jnp.exp(old - new) + (jnp.exp(a - new) + jnp.exp(b - new))

    ring(jnp.int32(0))
    step_a(jnp.int32(0))

    @pl.loop(1, 8)
    def _(k):
        pltpu.make_async_remote_copy(
            src_ref=lab_out, dst_ref=labs.at[z], send_sem=lsend, recv_sem=lrecv,
            device_id=dev((z + k) % 8, y, x, c), device_id_type=MESH).start()

    labs[z] = lab_out[...]

    def at_step(i, times, body):
        ready = [sum(1 for k in times if k // STEP_US < n) for n in range(STEPS + 1)]
        pl.loop(pick(i, ready[:-1]), pick(i, ready[1:]))(body)

    @pl.loop(0, STEPS)
    def _(i):
        at_step(i, RING, lambda n: ring(n + 1))
        at_step(i, SPREAD, lambda n: step_a(n + 1))
        at_step(i, SEND, w_first)
        at_step(i, ROUND1, step_b)
        at_step(i, DIRECT, w_direct)
        at_step(i, ROUND2, step_c)
        at_step(i, ACROSS, w_across)
        at_step(i, OTHER, w_other)

        @pl.when(i == 5)
        def _():
            seven = labs.at[pl.ds(0, 7)]
            pltpu.make_async_copy(seven, seven, lrecv).wait()
            pltpu.make_async_copy(seven, seven, lsend).wait()

            @pl.loop(0, 8)
            def _(d):
                pair = labs[z_of(d)]
                for k, size in ((0, 128), (1, 32)):
                    line = jnp.transpose(jnp.broadcast_to(pair[k : k + 1], (128, 128)))
                    labcol[pl.ds(pl.multiple_of(d * GROUP + k * 128, 32), size), :] = line[:size]

        at_step(
            i, [k[2] for k in CELLS],
            lambda n: cell(pick(n, [k[0] for k in CELLS]), pick(n, [k[1] for k in CELLS])))
        at_step(i, ROUND3, step_d)

    ids = lax.broadcasted_iota(jnp.int32, (128, 128), 1)

    def pack(d):
        columns = []
        for base, size in ((0, 128), (128, 32)):
            rows = pl.ds(d * GROUP + base, size)
            m = m_ref[rows, :]
            top = jnp.max(m, axis=1, keepdims=True)
            total = jnp.sum(s_ref[rows, :] * jnp.exp(m - top), axis=1, keepdims=True)
            got = jnp.sum(p_ref[rows, :], axis=1, keepdims=True)
            columns.append((top, total, got))
        packed = jnp.zeros((128, 128), jnp.float32)
        for k in range(3):
            packed = jnp.where(ids == 2 * k, columns[0][k], packed)
            fill = jnp.full((96, 1), 1.0 if k == 1 else 0.0, jnp.float32)
            packed = jnp.where(ids == 2 * k + 1, jnp.concatenate([columns[1][k], fill], axis=0), packed)
        out1[d] = jnp.transpose(packed)[:8]

    def to_owner(d):
        pltpu.make_async_remote_copy(
            src_ref=out1.at[d], dst_ref=in1.at[z], send_sem=fsend.at[0], recv_sem=frecv.at[0],
            device_id=dev(z_of(d), y, x, c), device_id_type=MESH).start()

    for k in range(5):
        if k < 4:
            cell(3 - k, NQ - 1)
        if k > 0:
            for d in (9 - 2 * k, 8 - 2 * k):
                pack(d)
            for d in (9 - 2 * k, 8 - 2 * k):
                if d > 0:
                    to_owner(d)

    in1[z] = out1[0]
    seven = in1.at[pl.ds(0, 7)]
    pltpu.make_async_copy(seven, seven, frecv.at[0]).wait()
    top, total, got = joined([in1[k] for k in range(8)])
    out2[0:2, :] = top
    out2[2:4, :] = total
    out2[4:6, :] = got
    out2[6:8, :] = got

    @pl.loop(20, 51)
    def _(k):
        pltpu.make_async_remote_copy(
            src_ref=out2, dst_ref=in2.at[v], send_sem=fsend.at[1], recv_sem=frecv.at[1],
            device_id={"dp": z, "vocab": (v + k + k // 32) % 32}, device_id_type=MESH).start()

    in2[v] = out2[...]
    many = in2.at[pl.ds(0, 31)]
    pltpu.make_async_copy(many, many, frecv.at[1]).wait()
    for pair in range(2):
        for core in range(2):
            tiles = [in2[((pair * 2 + k // 4) * 4 + k % 4) * 2 + core] for k in range(8)]
            top, total, got = joined(tiles)
            at = (pair * 2 + core) * 2
            loss_in[at : at + 2, :] = top + jnp.log(total) - got
    loss_sum = jnp.sum(mask_in[...] * loss_in[...], axis=(0, 1), keepdims=True)
    tally = jnp.sum(mask_in[...], axis=(0, 1), keepdims=True)
    out3[0:4, :] = jnp.broadcast_to(loss_sum, (4, 128))
    out3[4:8, :] = jnp.broadcast_to(tally, (4, 128))

    for k in (4, 3, 5, 2, 6, 1, 7):
        pltpu.make_async_remote_copy(
            src_ref=out3, dst_ref=in3.at[z], send_sem=fsend.at[2], recv_sem=frecv.at[2],
            device_id=dev((z + k) % 8, y, x, c), device_id_type=MESH).start()

    in3[z] = out3[...]
    losses = loss_in[...]
    for k in range(5):
        moved = lax.dot_general(
            losses, perm[k], (((1,), (1,)), ((), ())),
            preferred_element_type=jnp.float32, precision=lax.Precision.HIGHEST)
        loss_ref[k : k + 1, :] = jnp.sum(jnp.where(is_row(k), moved, 0.0), axis=0, keepdims=True)
    seven3 = in3.at[pl.ds(0, 7)]
    pltpu.make_async_copy(seven3, seven3, frecv.at[2]).wait()
    sums = functools.reduce(jnp.add, [in3[k] for k in range(8)])
    mean_ref[...] = sums[0:1, 0:1] / jnp.maximum(sums[4:5, 0:1], 1.0)

    pltpu.make_async_copy(seven, seven, fsend.at[0]).wait()
    pltpu.make_async_copy(many, many, fsend.at[1]).wait()
    pltpu.make_async_copy(seven3, seven3, fsend.at[2]).wait()
    hidden_bytes = wbuf.at[:, pl.ds(0, 63 * 64), :]
    pltpu.make_async_copy(hidden_bytes, hidden_bytes, hsend).wait()

    @pl.when(selfish)
    def _():
        part = wbuf.at[:, pl.ds(0, D - 256), :]
        pltpu.make_async_copy(part, part, wsend).wait()

    @pl.when(jnp.logical_not(selfish))
    def _():
        pltpu.make_async_copy(wbuf, wbuf, wsend).wait()


def scored(hidden, weight, labels, mask):
    vmem = pl.BlockSpec(memory_space=pltpu.VMEM)
    anywhere = pl.BlockSpec(memory_space=pl.ANY)
    return pl.pallas_call(
        main_kernel,
        out_shape=(jax.ShapeDtypeStruct((5, 128), jnp.float32), jax.ShapeDtypeStruct((1, 1), jnp.float32)),
        in_specs=[anywhere, anywhere, vmem, vmem],
        out_specs=(vmem, vmem),
        scratch_shapes=[
            pltpu.VMEM((TOK, D), jnp.bfloat16),
            pltpu.VMEM((64, 16, D // 4), jnp.bfloat16),
            pltpu.VMEM((NQ, D, 2 * CH), jnp.bfloat16),
            pltpu.VMEM((ROWS, D), jnp.bfloat16),
            pltpu.VMEM((5, 128, 128), jnp.float32),
            pltpu.VMEM((8, 128), jnp.int32),
            pltpu.VMEM((8, 128), jnp.float32),
            pltpu.VMEM((8, 128), jnp.float32),
            pltpu.VMEM((8, 8, 128), jnp.int32),
            pltpu.VMEM((TOK, 128), jnp.int32),
            pltpu.VMEM((16, D), jnp.float32),
            pltpu.VMEM((TOK, 128), jnp.float32),
            pltpu.VMEM((TOK, 128), jnp.float32),
            pltpu.VMEM((TOK, 128), jnp.float32),
            pltpu.VMEM((8, 8, 128), jnp.float32),
            pltpu.VMEM((8, 8, 128), jnp.float32),
            pltpu.VMEM((8, 128), jnp.float32),
            pltpu.VMEM((32, 8, 128), jnp.float32),
            pltpu.VMEM((8, 128), jnp.float32),
            pltpu.VMEM((8, 8, 128), jnp.float32),
            pltpu.SemaphoreType.DMA((64,)),
            pltpu.SemaphoreType.DMA,
            pltpu.SemaphoreType.DMA((NQ, 8, 2)),
            pltpu.SemaphoreType.DMA,
            pltpu.SemaphoreType.DMA,
            pltpu.SemaphoreType.DMA,
            pltpu.SemaphoreType.DMA,
            pltpu.SemaphoreType.DMA((3,)),
            pltpu.SemaphoreType.DMA((3,)),
        ],
        compiler_params=pltpu.CompilerParams(
            collective_id=0, has_side_effects=True, vmem_limit_bytes=60 * 2**20),
        name="gather_and_score",
    )(hidden, weight, labels, mask)


def shards(hidden, out_weight, labels, text_mask):
    loss, mean = scored(hidden, out_weight, labels.reshape(5, 128), text_mask.reshape(5, 128))
    return (text_mask.astype(jnp.float32) * loss.reshape(-1), mean[0, 0])


def solution(mesh):
    in_specs = (P(("dp", "vocab"), None), P("dp", "vocab"), P("dp"), P("dp"))
    out_specs = (P("dp"), P())
    return jax.shard_map(shards, mesh=mesh, in_specs=in_specs, out_specs=out_specs, check_vma=False)
```
